32 devices in a mesh: dp: 4 (over z), ctx: 8 (over y, x, core).
Axes of the slice: x: 2, y: 2, z: 4, core: 2. Of those that a mesh axis runs over, the one named last changes fastest.
Arguments:
- layer_input: bfloat16 [8, 1024, 1024], P('dp', 'ctx'), may hold values from -6 to 6
- qkv_weight: bfloat16 [1024, 3072], P('ctx'), may hold values from -0.1875 to 0.1875
- query_bias: float32 [1024], replicated, may hold values from -3 to 3
- value_bias: float32 [1024], replicated, may hold values from -3 to 3
- proj_weight: bfloat16 [1024, 1024], P('ctx'), may hold values from -3 to 3
- proj_bias: float32 [1024], replicated, may hold values from -3 to 3
- attn_gain: float32 [1024], replicated, may hold values from 0.1 to 1.9
- attn_shift: float32 [1024], replicated, may hold values from -3 to 3
- up_weight: bfloat16 [1024, 4096], P('ctx'), may hold values from -0.1875 to 0.1875
- up_bias: float32 [4096], replicated, may hold values from -3 to 3
- down_weight: bfloat16 [4096, 1024], P('ctx'), may hold values from -0.09375 to 0.09375
- down_bias: float32 [1024], replicated, may hold values from -3 to 3
- ffn_gain: float32 [1024], replicated, may hold values from 0.1 to 1.9
- ffn_shift: float32 [1024], replicated, may hold values from -3 to 3
- cotangent: bfloat16 [8, 1024, 1024], P('dp', 'ctx'), may hold values from -6 to 6
Outputs:
- layer_output: float32 [8, 1024, 1024], P('dp', 'ctx')
- input_grad: float32 [8, 1024, 1024], P('dp', 'ctx')
- qkv_weight_grad: float32 [1024, 3072], P('ctx')
- query_bias_grad: float32 [1024], replicated
- value_bias_grad: float32 [1024], replicated
- proj_weight_grad: float32 [1024, 1024], P('ctx')
- proj_bias_grad: float32 [1024], replicated
- attn_gain_grad: float32 [1024], replicated
- attn_shift_grad: float32 [1024], replicated
- up_weight_grad: float32 [1024, 4096], P('ctx')
- up_bias_grad: float32 [4096], replicated
- down_weight_grad: float32 [4096, 1024], P('ctx')
- down_bias_grad: float32 [1024], replicated
- ffn_gain_grad: float32 [1024], replicated
- ffn_shift_grad: float32 [1024], replicated
The draws below stay inside these ranges and needn't reach their ends.
All inputs are finite; a program needn't handle non-finite values.
Results may differ from the reference program's by a relative error of at most 0.012.
Values may be sent and summed in bfloat16 or wider, within the bound.
No kernel may reach another device: no remote copies, remote signals or barrier semaphores. Data moves between devices by JAX's collectives and lax.ppermute only.
A program may use at most 320 MiB of HBM per device.

```python
import math
import jax
import jax.numpy as jnp
from jax import lax

D = 1024
HEADS = 16
HEAD_DIM = 64
FF = 4096
LENGTH = 1024
NSEQ = 8


def steps_of(key, shape, cuts, least, largest):
    def one(position, shards_of):
        draws = jax.random.uniform(jax.random.fold_in(jax.random.fold_in(key, 6), position), (shards_of,), jnp.float32, least / len(cuts), largest / len(cuts))
        return jnp.repeat(jnp.exp(draws), shape[position] // shards_of).reshape((-1,) + (1,) * (len(shape) - position - 1))

    level = one(*cuts[0])
    for cut in cuts[1:]:
        level = level * one(*cut)
    return level


def scatter_about(stream_key, extent, scale, limit, cuts=(), kind=jnp.bfloat16):
    drawn = scale * jax.random.normal(stream_key, extent, jnp.float32)
    if cuts:
        drawn = drawn * steps_of(stream_key, extent, cuts, -0.22, 0.18)
    return jnp.clip(drawn, -limit, limit).astype(kind)


def setup_inputs(seed: int = 0) -> dict:
    streams_of = jax.random.split(jax.random.key(seed), 16)
    layer_input = scatter_about(streams_of[0], (NSEQ, LENGTH, D), 1.0, 6.0, ((0, 4), (1, 8)))
    qkv_weight = scatter_about(streams_of[1], (D, 3 * D), D ** -0.5, 0.1875, ((0, 8),))
    query_bias = scatter_about(streams_of[2], (D,), 0.5, 3.0, (), jnp.float32)
    value_bias = scatter_about(streams_of[3], (D,), 0.5, 3.0, (), jnp.float32)
    proj_weight = scatter_about(streams_of[4], (D, D), (max(D // 256, 1)) ** -0.5, 3.0, ((0, 8),))
    proj_bias = scatter_about(streams_of[5], (D,), 0.5, 3.0, (), jnp.float32)
    attn_gain = jnp.clip(1.0 + 0.18 * jax.random.normal(streams_of[6], (D,), jnp.float32), 0.1, 1.9)
    attn_shift = scatter_about(streams_of[7], (D,), 0.5, 3.0, (), jnp.float32)
    up_weight = scatter_about(streams_of[8], (D, FF), D ** -0.5, 0.1875, ((0, 8),))
    up_bias = scatter_about(streams_of[9], (FF,), 0.5, 3.0, (), jnp.float32)
    down_weight = scatter_about(streams_of[10], (FF, D), FF ** -0.5, 0.09375, ((0, 8),))
    down_bias = scatter_about(streams_of[11], (D,), 0.5, 3.0, (), jnp.float32)
    ffn_gain = jnp.clip(1.0 + 0.18 * jax.random.normal(streams_of[12], (D,), jnp.float32), 0.1, 1.9)
    ffn_shift = scatter_about(streams_of[13], (D,), 0.5, 3.0, (), jnp.float32)
    cotangent = scatter_about(streams_of[14], (NSEQ, LENGTH, D), 1.0, 6.0, ((0, 4), (1, 8)))
    return {"layer_input": layer_input, "qkv_weight": qkv_weight, "query_bias": query_bias, "value_bias": value_bias, "proj_weight": proj_weight, "proj_bias": proj_bias, "attn_gain": attn_gain, "attn_shift": attn_shift, "up_weight": up_weight, "up_bias": up_bias, "down_weight": down_weight, "down_bias": down_bias, "ffn_gain": ffn_gain, "ffn_shift": ffn_shift, "cotangent": cotangent}


@jax.custom_vjp
def low(v):
    return lax.optimization_barrier(v.astype(jnp.bfloat16)).astype(jnp.float32)

@jax.custom_vjp
def low_back(v):
    return v

def low_keep(v):
    return (low(v), None)

def low_pass(kept, grad):
    return (grad,)

def back_keep(v):
    return (v, None)

def back_low(kept, grad):
    return (low(grad),)
low.defvjp(low_keep, low_pass)
low_back.defvjp(back_keep, back_low)
EPS = 1e-05

def matmul(left, right):
    return jnp.dot(left, right, precision=lax.Precision.HIGHEST)

def layer_norm(values, gain, shift):
    center = values - lax.optimization_barrier(jnp.mean(values, -1, keepdims=True))
    spread = lax.optimization_barrier(jnp.mean(center * center, -1, keepdims=True))
    return center * lax.rsqrt(spread + EPS) * gain + shift

def attend(packed):
    query, key, value = packed
    scale = HEAD_DIM ** (-0.5)
    query_heads = query.reshape(LENGTH, HEADS, HEAD_DIM)
    key_heads = key.reshape(LENGTH, HEADS, HEAD_DIM)
    value_heads = value.reshape(LENGTH, HEADS, HEAD_DIM)
    block = math.gcd(LENGTH, 512)
    blocks = query_heads.reshape(LENGTH // block, block, HEADS, HEAD_DIM)

    def one_block(query_block):
        scores = low_back(jnp.einsum('qhd,khd->hqk', query_block, key_heads, precision=lax.Precision.HIGHEST) * scale)
        shifted = scores - lax.optimization_barrier(jnp.max(scores, -1, keepdims=True))
        expo = jnp.exp(shifted)
        probs = expo / lax.optimization_barrier(jnp.sum(expo, -1, keepdims=True))
        return jnp.einsum('hqk,khd->qhd', low(probs), value_heads, precision=lax.Precision.HIGHEST)
    return lax.map(jax.checkpoint(one_block), blocks).reshape(LENGTH, D)

def layer(layer_input, qkv_weight, query_bias, value_bias, proj_weight, proj_bias, attn_gain, attn_shift, up_weight, up_bias, down_weight, down_bias, ffn_gain, ffn_shift):
    flat_input = layer_input.reshape(-1, D)
    projected = matmul(flat_input, qkv_weight)
    query = low_back(low(projected[:, :D] + query_bias))
    key = low_back(low(projected[:, D:2 * D]))
    value = low_back(low(projected[:, 2 * D:] + value_bias))
    shape3 = (NSEQ, LENGTH, D)
    attn = lax.map(jax.checkpoint(attend), (query.reshape(shape3), key.reshape(shape3), value.reshape(shape3)))
    attn_low = low_back(low(attn.reshape(-1, D)))
    mixed = low_back(matmul(attn_low, proj_weight) + proj_bias)
    normed = layer_norm(flat_input + mixed, attn_gain, attn_shift)
    pre_act = low_back(matmul(low(normed), up_weight) + up_bias)
    activated = low(jax.nn.gelu(pre_act, approximate=False))
    branch = low_back(matmul(activated, down_weight) + down_bias)
    result = layer_norm(normed + branch, ffn_gain, ffn_shift)
    return result.reshape(shape3)

def reference(layer_input, qkv_weight, query_bias, value_bias, proj_weight, proj_bias, attn_gain, attn_shift, up_weight, up_bias, down_weight, down_bias, ffn_gain, ffn_shift, cotangent):
    inputs = [item.astype(jnp.float32) for item in (layer_input, qkv_weight, query_bias, value_bias, proj_weight, proj_bias, attn_gain, attn_shift, up_weight, up_bias, down_weight, down_bias, ffn_gain, ffn_shift)]
    output, pull = jax.vjp(layer, *inputs)
    grads = pull(cotangent.astype(jnp.float32))
    return (output, grads[0], grads[1], grads[2], grads[3], grads[4], grads[5], grads[6], grads[7], grads[8], grads[9], grads[10], grads[11], grads[12], grads[13])
```

```python
import functools
import math

import jax
import jax.numpy as jnp
from jax import lax
from jax.experimental import pallas as pl
from jax.experimental.pallas import tpu as pltpu
from jax.sharding import PartitionSpec as P

HEADS = 16


EPS = 1e-05
NEGATIVE = -1e30


def layer_norm(values, gain, shift):
    center = values - jnp.mean(values, -1, keepdims=True)
    spread = jnp.mean(center * center, -1, keepdims=True)
    return center * lax.rsqrt(spread + EPS) * gain + shift


def exact_gelu(values):
    return jax.nn.gelu(values, approximate=False)


def left_dot(left, right):
    return lax.dot_general(
        left, right, (((0,), (0,)), ((), ())), preferred_element_type=jnp.float32
    )


def right_dot(left, right):
    return lax.dot_general(
        left, right, (((1,), (1,)), ((), ())), preferred_element_type=jnp.float32
    )


def split_heads(values, heads):
    return values.reshape(values.shape[0], values.shape[1], heads, values.shape[2] // heads)


def row_blocks(values, block):
    shaped = values.reshape((values.shape[0], values.shape[1] // block, block) + values.shape[2:])
    return jnp.moveaxis(shaped, 1, 0)


def per_device(
    layer_input,
    qkv_weight,
    query_bias,
    value_bias,
    proj_weight,
    proj_bias,
    attn_gain,
    attn_shift,
    up_weight,
    up_bias,
    down_weight,
    down_bias,
    ffn_gain,
    ffn_shift,
    cotangent,
):
    seq_count, span_rows, width = layer_input.shape
    heads = HEADS
    head_size = width // heads
    scale = head_size ** (-0.5)
    shape_local = (seq_count, span_rows, width)
    qkv_full, proj_full, up_full, down_full = (
        lax.all_gather(qkv_weight, "ctx", axis=0, tiled=True),
        lax.all_gather(proj_weight, "ctx", axis=0, tiled=True),
        lax.all_gather(up_weight, "ctx", axis=0, tiled=True),
        lax.all_gather(down_weight, "ctx", axis=0, tiled=True),
    )
    flat_input = layer_input.reshape(-1, width)
    projected = jnp.dot(flat_input, qkv_full, preferred_element_type=jnp.float32)
    query_rows = (projected[:, :width] + query_bias).astype(jnp.bfloat16)
    key_rows = projected[:, width : 2 * width].astype(jnp.bfloat16)
    value_rows = (projected[:, 2 * width :] + value_bias).astype(jnp.bfloat16)
    query_local = query_rows.reshape(shape_local)
    key_local = key_rows.reshape(shape_local)
    value_local = value_rows.reshape(shape_local)
    query_heads = split_heads(query_local, heads)
    key_heads = split_heads(key_local, heads)
    value_heads = split_heads(value_local, heads)
    total_start = (
        jnp.full((seq_count, heads, span_rows), NEGATIVE, jnp.float32),
        jnp.zeros((seq_count, heads, span_rows), jnp.float32),
    )
    accum_start = jnp.zeros((seq_count, heads, span_rows, head_size), jnp.float32)
    piece = lax.all_gather(key_local, "ctx", axis=1, tiled=True)
    block = math.gcd(piece.shape[1], 512)

    def total_inner(state, key_part):
        running, total = state
        key_block = split_heads(key_part, heads)
        scores = (
            jnp.einsum(
                "sqhd,skhd->shqk", query_heads, key_block, preferred_element_type=jnp.float32
            )
            * scale
        )
        newest = jnp.maximum(running, jnp.max(scores, -1))
        total = total * jnp.exp(running - newest) + jnp.sum(jnp.exp(scores - newest[..., None]), -1)
        return ((newest, total), None)

    result, unused = lax.scan(total_inner, total_start, row_blocks(piece, block))
    running, total = result
    log_total = running + jnp.log(total)
    piece = (
        lax.all_gather(key_local, "ctx", axis=1, tiled=True),
        lax.all_gather(value_local, "ctx", axis=1, tiled=True),
    )
    block = math.gcd(piece[0].shape[1], 512)

    def value_inner(accum, pair):
        key_block = split_heads(pair[0], heads)
        value_block = split_heads(pair[1], heads)
        scores = (
            jnp.einsum(
                "sqhd,skhd->shqk", query_heads, key_block, preferred_element_type=jnp.float32
            )
            * scale
        )
        weights = jnp.exp(scores - log_total[..., None]).astype(jnp.bfloat16)
        accum = accum + jnp.einsum(
            "shqk,skhd->shqd", weights, value_block, preferred_element_type=jnp.float32
        )
        return (accum, None)

    result, unused = lax.scan(
        value_inner, accum_start, (row_blocks(piece[0], block), row_blocks(piece[1], block))
    )
    accum = result
    attn_heads = jnp.moveaxis(accum, 1, 2)
    attn_rows = attn_heads.reshape(-1, width).astype(jnp.bfloat16)
    mixed = jnp.dot(attn_rows, proj_full, preferred_element_type=jnp.float32) + proj_bias
    first_sum = flat_input.astype(jnp.float32) + mixed
    normed, first_pull = jax.vjp(layer_norm, first_sum, attn_gain, attn_shift)
    normed_low = normed.astype(jnp.bfloat16)
    pre_act = jnp.dot(normed_low, up_full, preferred_element_type=jnp.float32) + up_bias
    activated, gelu_pull = jax.vjp(exact_gelu, pre_act)
    act_low = activated.astype(jnp.bfloat16)
    branch = jnp.dot(act_low, down_full, preferred_element_type=jnp.float32) + down_bias
    result_rows, second_pull = jax.vjp(layer_norm, normed + branch, ffn_gain, ffn_shift)
    layer_output = result_rows.reshape(shape_local)
    grad_out = cotangent.reshape(-1, width).astype(jnp.float32)
    grad_second, ffn_gain_grad, ffn_shift_grad = second_pull(grad_out)
    qkv_back, proj_back, up_back, down_back = (
        lax.all_gather(qkv_weight, "ctx", axis=0, tiled=True),
        lax.all_gather(proj_weight, "ctx", axis=0, tiled=True),
        lax.all_gather(up_weight, "ctx", axis=0, tiled=True),
        lax.all_gather(down_weight, "ctx", axis=0, tiled=True),
    )
    grad_branch = grad_second.astype(jnp.bfloat16)
    down_weight_local = left_dot(act_low, grad_branch)
    down_bias_grad = jnp.sum(grad_branch.astype(jnp.float32), 0)
    grad_act = right_dot(grad_branch, down_back)
    grad_pre = gelu_pull(grad_act)[0].astype(jnp.bfloat16)
    up_weight_local = left_dot(normed_low, grad_pre)
    up_bias_grad = jnp.sum(grad_pre.astype(jnp.float32), 0)
    grad_normed = grad_second + right_dot(grad_pre, up_back)
    grad_first, attn_gain_grad, attn_shift_grad = first_pull(grad_normed)
    grad_mixed = grad_first.astype(jnp.bfloat16)
    proj_weight_local = left_dot(attn_rows, grad_mixed)
    proj_bias_grad = jnp.sum(grad_mixed.astype(jnp.float32), 0)
    grad_attn = right_dot(grad_mixed, proj_back).astype(jnp.bfloat16).reshape(shape_local)
    grad_attn_heads = split_heads(grad_attn, heads)
    delta_local = jnp.sum(grad_attn_heads.astype(jnp.float32) * attn_heads, -1)
    delta_heads = jnp.moveaxis(delta_local, 2, 1)
    query_start = jnp.zeros((seq_count, span_rows, heads, head_size), jnp.float32)
    piece = (
        lax.all_gather(key_local, "ctx", axis=1, tiled=True),
        lax.all_gather(value_local, "ctx", axis=1, tiled=True),
    )
    block = math.gcd(piece[0].shape[1], 512)

    def query_inner(accum, pair):
        key_block = split_heads(pair[0], heads)
        value_block = split_heads(pair[1], heads)
        scores = (
            jnp.einsum(
                "sqhd,skhd->shqk", query_heads, key_block, preferred_element_type=jnp.float32
            )
            * scale
        )
        probs = jnp.exp(scores - log_total[..., None])
        grad_probs = jnp.einsum(
            "sqhd,skhd->shqk", grad_attn_heads, value_block, preferred_element_type=jnp.float32
        )
        grad_scores = (probs * (grad_probs - delta_heads[..., None])).astype(jnp.bfloat16)
        accum = (
            accum
            + jnp.einsum(
                "shqk,skhd->sqhd", grad_scores, key_block, preferred_element_type=jnp.float32
            )
            * scale
        )
        return (accum, None)

    result, unused = lax.scan(
        query_inner, query_start, (row_blocks(piece[0], block), row_blocks(piece[1], block))
    )
    grad_query = result
    lse_all, delta_all = (
        lax.all_gather(jnp.moveaxis(log_total, 1, 2), "ctx", axis=1, tiled=True),
        lax.all_gather(delta_local, "ctx", axis=1, tiled=True),
    )
    key_start = (
        jnp.zeros((seq_count, span_rows, heads, head_size), jnp.float32),
        jnp.zeros((seq_count, span_rows, heads, head_size), jnp.float32),
    )
    piece = (
        lax.all_gather(query_local, "ctx", axis=1, tiled=True),
        lax.all_gather(grad_attn, "ctx", axis=1, tiled=True),
    )
    count = piece[0].shape[1]
    block = math.gcd(count, 512)

    def key_inner(state, group):
        grad_key, grad_value = state
        query_block = split_heads(group[0], heads)
        grad_block = split_heads(group[1], heads)
        lse_block = jnp.moveaxis(group[2], 2, 1)
        delta_block = jnp.moveaxis(group[3], 2, 1)
        scores = (
            jnp.einsum(
                "sqhd,skhd->shqk", query_block, key_heads, preferred_element_type=jnp.float32
            )
            * scale
        )
        probs = jnp.exp(scores - lse_block[..., None])
        grad_value = grad_value + jnp.einsum(
            "shqk,sqhd->skhd",
            probs.astype(jnp.bfloat16),
            grad_block,
            preferred_element_type=jnp.float32,
        )
        grad_probs = jnp.einsum(
            "sqhd,skhd->shqk", grad_block, value_heads, preferred_element_type=jnp.float32
        )
        grad_scores = (probs * (grad_probs - delta_block[..., None])).astype(jnp.bfloat16)
        grad_key = (
            grad_key
            + jnp.einsum(
                "shqk,sqhd->skhd", grad_scores, query_block, preferred_element_type=jnp.float32
            )
            * scale
        )
        return ((grad_key, grad_value), None)

    members = (
        row_blocks(piece[0], block),
        row_blocks(piece[1], block),
        row_blocks(lse_all, block),
        row_blocks(delta_all, block),
    )
    result, unused = lax.scan(key_inner, key_start, members)
    grad_key, grad_value = result
    grad_query_rows = grad_query.reshape(-1, width).astype(jnp.bfloat16)
    grad_key_rows = grad_key.reshape(-1, width).astype(jnp.bfloat16)
    grad_value_rows = grad_value.reshape(-1, width).astype(jnp.bfloat16)
    grad_qkv = jnp.concatenate([grad_query_rows, grad_key_rows, grad_value_rows], 1)
    qkv_weight_local = left_dot(flat_input, grad_qkv)
    query_bias_grad = jnp.sum(grad_query_rows.astype(jnp.float32), 0)
    value_bias_grad = jnp.sum(grad_value_rows.astype(jnp.float32), 0)
    input_grad = (grad_first + right_dot(grad_qkv, qkv_back)).reshape(shape_local)
    shard_grads = (
        lax.psum_scatter(qkv_weight_local, "ctx", scatter_dimension=0, tiled=True),
        lax.psum_scatter(proj_weight_local, "ctx", scatter_dimension=0, tiled=True),
        lax.psum_scatter(up_weight_local, "ctx", scatter_dimension=0, tiled=True),
        lax.psum_scatter(down_weight_local, "ctx", scatter_dimension=0, tiled=True),
    )
    qkv_weight_grad, proj_weight_grad, up_weight_grad, down_weight_grad = lax.psum(
        (shard_grads[0], shard_grads[1], shard_grads[2], shard_grads[3]), "dp"
    )
    small_summed = lax.psum(
        (
            query_bias_grad,
            value_bias_grad,
            proj_bias_grad,
            attn_gain_grad,
            attn_shift_grad,
            up_bias_grad,
            down_bias_grad,
            ffn_gain_grad,
            ffn_shift_grad,
        ),
        ("dp", "ctx"),
    )
    return (
        layer_output,
        input_grad,
        qkv_weight_grad,
        small_summed[0],
        small_summed[1],
        proj_weight_grad,
        small_summed[2],
        small_summed[3],
        small_summed[4],
        up_weight_grad,
        small_summed[5],
        down_weight_grad,
        small_summed[6],
        small_summed[7],
        small_summed[8],
    )


def choose_plan(mesh):
    size = mesh.shape["ctx"]
    groups = mesh.shape["dp"]
    packed = size >= 4 and size & (size - 1) == 0 and HEADS % size == 0
    if not packed or groups != 4:
        return per_device
    return functools.partial(head_parallel, size, groups)


def exchange(values, size, bits):
    return lax.ppermute(values, "ctx", [(spot, spot ^ bits) for spot in range(size)])


def block_order(size):
    return [2 * spot for spot in range(size // 2)] + [2 * spot + 1 for spot in range(size // 2)]


def link_bits(size):
    bits = []
    step = 2
    while step < size:
        bits.append(step)
        step *= 2
    return bits


def gather_blocks(values, size):
    rows = values.shape[0]
    half = rows // 2
    parts = []
    for piece, bits in (
        (values[:half], link_bits(size)),
        (values[half:], link_bits(size)[::-1]),
    ):
        held = {0: piece}
        for bit in bits:
            labels = sorted(held)
            moved = exchange(jnp.stack([held[label] for label in labels]), size, bit)
            for spot, label in enumerate(labels):
                held[label | bit] = moved[spot]
        parts.append(held)
    near = jnp.concatenate(
        [part[label] for label in block_order(size)[: size // 2] for part in parts], 0
    )
    return jnp.concatenate([near, exchange(near, size, 1)], 0)


def scatter_blocks(values, size):
    order = block_order(size)
    rows = values.shape[0] // size
    half = rows // 2
    near_rows = values.shape[0] // 2
    moved = exchange(values[near_rows:], size, 1)
    near = values[:near_rows].astype(jnp.float32) + moved.astype(jnp.float32)
    near = near.astype(jnp.bfloat16).reshape(size // 2, rows, values.shape[1])
    outs = []
    for low, bits in ((0, link_bits(size)[::-1]), (half, link_bits(size))):
        held = {label: near[spot, low : low + half] for spot, label in enumerate(order[: size // 2])}
        for bit in bits:
            send = sorted(label for label in held if label & bit)
            keep = [label ^ bit for label in send]
            moved = exchange(jnp.stack([held[label] for label in send]), size, bit)
            total = {}
            for spot, label in enumerate(keep):
                summed = held[label].astype(jnp.float32) + moved[spot].astype(jnp.float32)
                total[label] = summed if bit == bits[-1] else summed.astype(jnp.bfloat16)
            held = total
        outs.append(held[0])
    return jnp.concatenate(outs, 0)


def trade_blocks(blocks, size):
    return [blocks[0]] + [exchange(blocks[bits], size, bits) for bits in range(1, size)]


def trade_columns(values, size, me):
    blocks = [
        lax.dynamic_index_in_dim(values, me ^ bits, 0, keepdims=False) for bits in range(size)
    ]
    got = jnp.stack(trade_blocks(blocks, size))
    return jnp.stack(
        [lax.dynamic_index_in_dim(got, me ^ spot, 0, keepdims=False) for spot in range(size)]
    )


def group_sum(values, chunks):
    spot = lax.axis_index("dp")
    end = (spot == 0) | (spot == 3)
    outs = []
    gate = None
    for piece in jnp.split(values, chunks, 0):
        if gate is not None:
            piece, gate = lax.optimization_barrier((piece, gate))
        got = lax.ppermute(piece, "dp", [(0, 1), (3, 2)])
        gate = got
        pair = (piece.astype(jnp.float32) + got.astype(jnp.float32)).astype(jnp.bfloat16)
        other = lax.ppermute(pair, "dp", [(1, 2), (2, 1)])
        total = (pair.astype(jnp.float32) + other.astype(jnp.float32)).astype(jnp.bfloat16)
        last = lax.ppermute(total, "dp", [(1, 0), (2, 3)])
        outs.append(jnp.where(end, last, total))
    return jnp.concatenate(outs, 0) if len(outs) > 1 else outs[0]


def small_sum(values, size, groups):
    step = 1
    while step < size:
        values = values + exchange(values, size, step)
        step *= 2
    step = 1
    while step < groups:
        values = values + lax.ppermute(values, "dp", [(g, g ^ step) for g in range(groups)])
        step *= 2
    return values


def attend_kernel(head_size, scale, q_ref, k_ref, v_ref, out_ref, lse_ref):
    lanes = q_ref.shape[1]
    head_of = lax.broadcasted_iota(jnp.int32, (1, lanes), 1) // head_size
    query = q_ref[...]
    total = jnp.zeros((lanes, query.shape[0]), jnp.float32)
    for head in range(lanes // head_size):
        mine = head_of == head
        key = jnp.where(mine, k_ref[...], jnp.zeros_like(k_ref))
        value = jnp.where(mine, v_ref[...], jnp.zeros_like(v_ref))
        scores = right_dot(key, query) * scale
        top = jnp.max(scores, 0, keepdims=True)
        expo = jnp.exp(scores - top)
        norm = jnp.sum(expo, 0, keepdims=True)
        lse_ref[head : head + 1, :] = top + jnp.log(norm)
        total = total + left_dot(value, expo.astype(jnp.bfloat16)) / norm
    out_ref[...] = total.T.astype(jnp.bfloat16)


def attend(qkv, head_size, scale, block):
    rows = qkv.shape[0]
    lanes = qkv.shape[1] // 3
    heads = lanes // head_size
    return pl.pallas_call(
        functools.partial(attend_kernel, head_size, scale),
        grid=(rows // block,),
        in_specs=[
            pl.BlockSpec((block, lanes), lambda i: (i, 0)),
            pl.BlockSpec((rows, lanes), lambda i: (0, 1)),
            pl.BlockSpec((rows, lanes), lambda i: (0, 2)),
        ],
        out_specs=[
            pl.BlockSpec((block, lanes), lambda i: (i, 0)),
            pl.BlockSpec((heads, block), lambda i: (0, i)),
        ],
        out_shape=[
            jax.ShapeDtypeStruct((rows, lanes), jnp.bfloat16),
            jax.ShapeDtypeStruct((heads, rows), jnp.float32),
        ],
        cost_estimate=pl.CostEstimate(
            flops=4 * rows * rows * lanes * heads,
            bytes_accessed=8 * rows * lanes,
            transcendentals=rows * rows * heads,
        ),
        name="attend",
    )(qkv, qkv, qkv)


def attend_back_kernel(
    head_size, scale, q_ref, k_ref, v_ref, lse_ref, grad_ref, out_ref, gk_ref, gv_ref
):
    step = pl.program_id(0)
    block, lanes = q_ref.shape
    head_of = lax.broadcasted_iota(jnp.int32, (1, lanes), 1) // head_size
    query = q_ref[...]
    grad = grad_ref[...]

    @pl.when(step == 0)
    def _():
        gk_ref[...] = jnp.zeros_like(gk_ref)
        gv_ref[...] = jnp.zeros_like(gv_ref)

    total = jnp.zeros((lanes, block), jnp.float32)
    for head in range(lanes // head_size):
        mine = head_of == head
        key = jnp.where(mine, k_ref[...], jnp.zeros_like(k_ref))
        value = jnp.where(mine, v_ref[...], jnp.zeros_like(v_ref))
        query_head = jnp.where(mine, query, jnp.zeros_like(query))
        grad_head = jnp.where(mine, grad, jnp.zeros_like(grad))
        scores = right_dot(key, query) * scale
        probs = jnp.exp(scores - lse_ref[head : head + 1, :])
        grad_probs = right_dot(value, grad)
        gv_ref[...] += jnp.dot(
            probs.astype(jnp.bfloat16), grad_head, preferred_element_type=jnp.float32
        )
        delta = jnp.sum(probs * grad_probs, 0, keepdims=True)
        grad_scores = (probs * (grad_probs - delta)).astype(jnp.bfloat16)
        gk_ref[...] += jnp.dot(grad_scores, query_head, preferred_element_type=jnp.float32)
        total = total + left_dot(key, grad_scores)
    rows = pl.ds(pl.multiple_of(step * block, block), block)
    out_ref[rows, 0:lanes] = (total.T * scale).astype(jnp.bfloat16)

    @pl.when(step == pl.num_programs(0) - 1)
    def _():
        out_ref[:, lanes : 2 * lanes] = (gk_ref[...] * scale).astype(jnp.bfloat16)
        out_ref[:, 2 * lanes :] = gv_ref[...].astype(jnp.bfloat16)


def attend_back(qkv, lse, grad, head_size, scale, block):
    rows = qkv.shape[0]
    lanes = qkv.shape[1] // 3
    heads = lanes // head_size
    return pl.pallas_call(
        functools.partial(attend_back_kernel, head_size, scale),
        grid=(rows // block,),
        in_specs=[
            pl.BlockSpec((block, lanes), lambda i: (i, 0)),
            pl.BlockSpec((rows, lanes), lambda i: (0, 1)),
            pl.BlockSpec((rows, lanes), lambda i: (0, 2)),
            pl.BlockSpec((heads, block), lambda i: (0, i)),
            pl.BlockSpec((block, lanes), lambda i: (i, 0)),
        ],
        out_specs=pl.BlockSpec((rows, 3 * lanes), lambda i: (0, 0)),
        out_shape=jax.ShapeDtypeStruct((rows, 3 * lanes), jnp.bfloat16),
        scratch_shapes=[
            pltpu.VMEM((rows, lanes), jnp.float32),
            pltpu.VMEM((rows, lanes), jnp.float32),
        ],
        cost_estimate=pl.CostEstimate(
            flops=10 * rows * rows * lanes * heads,
            bytes_accessed=16 * rows * lanes,
            transcendentals=rows * rows * heads,
        ),
        name="attend_back",
    )(qkv, qkv, qkv, lse, grad)


def norm_parts(values):
    center = values - jnp.mean(values, -1, keepdims=True)
    spread = jnp.mean(center * center, -1, keepdims=True)
    inverse = lax.rsqrt(spread + EPS)
    return center * inverse, inverse


def norm_back(grad, hat, inverse, gain):
    grad_hat = grad * gain
    first = jnp.mean(grad_hat, -1, keepdims=True)
    second = jnp.mean(grad_hat * hat, -1, keepdims=True)
    return inverse * (grad_hat - first - hat * second)


def gelu_pair(values):
    area = 0.5 * (1.0 + lax.erf(values * (0.5**0.5)))
    density = jnp.exp(-0.5 * values * values) * (1.0 / math.sqrt(2.0 * math.pi))
    return values * area, area + values * density


def to_bf16(values):
    return values.astype(jnp.bfloat16)


def head_parallel(
    size,
    groups,
    layer_input,
    qkv_weight,
    query_bias,
    value_bias,
    proj_weight,
    proj_bias,
    attn_gain,
    attn_shift,
    up_weight,
    up_bias,
    down_weight,
    down_bias,
    ffn_gain,
    ffn_shift,
    cotangent,
):
    me = lax.axis_index("ctx")
    seq_count, span_rows, width = layer_input.shape
    hidden = up_weight.shape[1]
    lanes = width // size
    part = hidden // size
    head_size = width // HEADS
    scale = head_size ** (-0.5)
    length = span_rows * size
    block = math.gcd(length, 256)
    seqs = range(seq_count)
    order = block_order(size)

    qkv_blocks = jnp.moveaxis(qkv_weight.reshape(-1, 3, size, lanes), 2, 0)
    qkv_mine = trade_columns(qkv_blocks.reshape(size, -1, 3 * lanes), size, me)
    qkv_mine = qkv_mine.reshape(width, 3 * lanes)
    inputs = [gather_blocks(layer_input[s], size) for s in seqs]
    proj_all = gather_blocks(proj_weight, size)
    up_blocks = jnp.moveaxis(up_weight.reshape(-1, size, part), 1, 0)
    up_mine = trade_columns(up_blocks, size, me).reshape(width, part)
    qkv_bias = jnp.concatenate(
        [
            lax.dynamic_slice_in_dim(query_bias, me * lanes, lanes),
            jnp.zeros((lanes,), jnp.float32),
            lax.dynamic_slice_in_dim(value_bias, me * lanes, lanes),
        ]
    )
    up_bias_mine = lax.dynamic_slice_in_dim(up_bias, me * part, part)

    qkvs, lses, attns = [], [], []
    for s in seqs:
        qkv = to_bf16(jnp.dot(inputs[s], qkv_mine, preferred_element_type=jnp.float32) + qkv_bias)
        attn, lse = attend(qkv, head_size, scale, block)
        attn = attn.reshape(size, span_rows, lanes)
        got = trade_blocks([attn[order.index(r)] for r in range(size)], size)
        attns.append(jnp.concatenate([got[r] for r in order], 1))
        qkvs.append(qkv)
        lses.append(lse)

    normeds, lows, hats, inverses, slopes, acts, branches = [], [], [], [], [], [], []
    for s in seqs:
        mixed = jnp.dot(attns[s], proj_all, preferred_element_type=jnp.float32) + proj_bias
        hat, inverse = norm_parts(layer_input[s].astype(jnp.float32) + mixed)
        normed = hat * attn_gain + attn_shift
        low = gather_blocks(to_bf16(normed), size)
        pre = jnp.dot(low, up_mine, preferred_element_type=jnp.float32) + up_bias_mine
        act, slope = gelu_pair(pre)
        act = to_bf16(act)
        branch = to_bf16(jnp.dot(act, down_weight, preferred_element_type=jnp.float32))
        branches.append(scatter_blocks(branch, size))
        normeds.append(normed)
        lows.append(low)
        hats.append(hat)
        inverses.append(inverse)
        acts.append(act)
        slopes.append(to_bf16(slope))

    outputs, seconds, grad_branches, smalls = [], [], [], []
    for s in seqs:
        hat, inverse = norm_parts(normeds[s] + (branches[s] + down_bias))
        outputs.append(hat * ffn_gain + ffn_shift)
        grad = cotangent[s].astype(jnp.float32)
        second = norm_back(grad, hat, inverse, ffn_gain)
        low = to_bf16(second)
        smalls.append(
            [
                jnp.sum(grad * hat, 0),
                jnp.sum(grad, 0),
                jnp.sum(low.astype(jnp.float32), 0),
            ]
        )
        seconds.append(second)
        grad_branches.append(gather_blocks(low, size))

    down_grad, up_grad, up_bias_part = 0.0, 0.0, 0.0
    grad_normeds = []
    for s in seqs:
        grad_act = right_dot(grad_branches[s], down_weight)
        pre = to_bf16(grad_act * slopes[s].astype(jnp.float32))
        grad_normeds.append(scatter_blocks(to_bf16(right_dot(pre, up_mine)), size))
        down_grad = down_grad + left_dot(acts[s], grad_branches[s])
        up_grad = up_grad + left_dot(lows[s], pre)
        up_bias_part = up_bias_part + jnp.sum(pre.astype(jnp.float32), 0)

    down_weight_grad = group_sum(to_bf16(down_grad), 2).astype(jnp.float32)
    up_traded = trade_columns(to_bf16(up_grad).reshape(size, -1, part), size, me)
    up_weight_grad = group_sum(up_traded, 2).astype(jnp.float32)
    up_weight_grad = jnp.moveaxis(up_weight_grad, 0, 1).reshape(-1, hidden)

    firsts, grad_mixeds, grad_attns = [], [], []
    proj_grad = 0.0
    for s in seqs:
        grad_normed = seconds[s] + grad_normeds[s]
        first = norm_back(grad_normed, hats[s], inverses[s], attn_gain)
        low = to_bf16(first)
        smalls[s] += [
            jnp.sum(grad_normed * hats[s], 0),
            jnp.sum(grad_normed, 0),
            jnp.sum(low.astype(jnp.float32), 0),
        ]
        grad_attn = to_bf16(right_dot(low, proj_all))
        blocks = [grad_attn[:, k * lanes : (k + 1) * lanes] for k in range(size)]
        got = trade_blocks([blocks[order.index(r)] for r in range(size)], size)
        grad_attns.append(jnp.concatenate([got[r] for r in order], 0))
        proj_grad = proj_grad + left_dot(attns[s], low)
        firsts.append(first)

    qkv_grad = 0.0
    bias_part = 0.0
    input_grads = []
    for s in seqs:
        grad_qkv = attend_back(qkvs[s], lses[s], grad_attns[s], head_size, scale, block)
        input_grads.append(
            firsts[s] + scatter_blocks(to_bf16(right_dot(grad_qkv, qkv_mine)), size)
        )
        qkv_grad = qkv_grad + left_dot(inputs[s], grad_qkv)
        bias_part = bias_part + jnp.sum(grad_qkv.astype(jnp.float32), 0)

    qkv_traded = trade_columns(to_bf16(qkv_grad).reshape(size, -1, 3 * lanes), size, me)
    qkv_weight_grad = group_sum(qkv_traded, 4).astype(jnp.float32)
    qkv_weight_grad = jnp.moveaxis(qkv_weight_grad.reshape(size, -1, 3, lanes), 0, 2)
    qkv_weight_grad = qkv_weight_grad.reshape(-1, 3 * width)
    proj_weight_grad = group_sum(to_bf16(scatter_blocks(to_bf16(proj_grad), size)), 1)
    proj_weight_grad = proj_weight_grad.astype(jnp.float32)

    local = [sum(small[k] for small in smalls) for k in range(6)]
    placed = lax.dynamic_update_slice(jnp.zeros((hidden,), jnp.float32), up_bias_part, (me * part,))
    early = small_sum(jnp.concatenate(local + [placed]).reshape(-1, 128), size, groups).reshape(-1)
    zeros = jnp.zeros((width,), jnp.float32)
    late = jnp.concatenate(
        [
            lax.dynamic_update_slice(zeros, bias_part[:lanes], (me * lanes,)),
            lax.dynamic_update_slice(zeros, bias_part[2 * lanes :], (me * lanes,)),
        ]
    )
    late = small_sum(late.reshape(-1, 128), size, groups).reshape(-1)
    rows = [early[k * width : (k + 1) * width] for k in range(6)]
    return (
        jnp.stack(outputs),
        jnp.stack(input_grads),
        qkv_weight_grad,
        late[:width],
        late[width:],
        proj_weight_grad,
        rows[5],
        rows[3],
        rows[4],
        up_weight_grad,
        early[6 * width :],
        down_weight_grad,
        rows[2],
        rows[0],
        rows[1],
    )


def solution(mesh):
    return jax.shard_map(
        choose_plan(mesh),
        mesh=mesh,
        in_specs=(
            P("dp", "ctx", None),
            P("ctx", None),
            P(),
            P(),
            P("ctx", None),
            P(),
            P(),
            P(),
            P("ctx", None),
            P(),
            P("ctx", None),
            P(),
            P(),
            P(),
            P("dp", "ctx", None),
        ),
        out_specs=(
            P("dp", "ctx", None),
            P("dp", "ctx", None),
            P("ctx", None),
            P(),
            P(),
            P("ctx", None),
            P(),
            P(),
            P(),
            P("ctx", None),
            P(),
            P("ctx", None),
            P(),
            P(),
            P(),
        ),
        check_vma=False,
    )
```

```python
import functools
import math

import jax
import jax.numpy as jnp
from jax import lax
from jax.experimental import pallas as pl
from jax.experimental.pallas import tpu as pltpu
from jax.sharding import PartitionSpec as P

HEADS = 16


EPS = 1e-05
NEGATIVE = -1e30


def layer_norm(values, gain, shift):
    center = values - jnp.mean(values, -1, keepdims=True)
    spread = jnp.mean(center * center, -1, keepdims=True)
    return center * lax.rsqrt(spread + EPS) * gain + shift


def exact_gelu(values):
    return jax.nn.gelu(values, approximate=False)


def left_dot(left, right):
    return lax.dot_general(
        left, right, (((0,), (0,)), ((), ())), preferred_element_type=jnp.float32
    )


def right_dot(left, right):
    return lax.dot_general(
        left, right, (((1,), (1,)), ((), ())), preferred_element_type=jnp.float32
    )


def split_heads(values, heads):
    return values.reshape(values.shape[0], values.shape[1], heads, values.shape[2] // heads)


def row_blocks(values, block):
    shaped = values.reshape((values.shape[0], values.shape[1] // block, block) + values.shape[2:])
    return jnp.moveaxis(shaped, 1, 0)


def per_device(
    layer_input,
    qkv_weight,
    query_bias,
    value_bias,
    proj_weight,
    proj_bias,
    attn_gain,
    attn_shift,
    up_weight,
    up_bias,
    down_weight,
    down_bias,
    ffn_gain,
    ffn_shift,
    cotangent,
):
    seq_count, span_rows, width = layer_input.shape
    heads = HEADS
    head_size = width // heads
    scale = head_size ** (-0.5)
    shape_local = (seq_count, span_rows, width)
    qkv_full, proj_full, up_full, down_full = (
        lax.all_gather(qkv_weight, "ctx", axis=0, tiled=True),
        lax.all_gather(proj_weight, "ctx", axis=0, tiled=True),
        lax.all_gather(up_weight, "ctx", axis=0, tiled=True),
        lax.all_gather(down_weight, "ctx", axis=0, tiled=True),
    )
    flat_input = layer_input.reshape(-1, width)
    projected = jnp.dot(flat_input, qkv_full, preferred_element_type=jnp.float32)
    query_rows = (projected[:, :width] + query_bias).astype(jnp.bfloat16)
    key_rows = projected[:, width : 2 * width].astype(jnp.bfloat16)
    value_rows = (projected[:, 2 * width :] + value_bias).astype(jnp.bfloat16)
    query_local = query_rows.reshape(shape_local)
    key_local = key_rows.reshape(shape_local)
    value_local = value_rows.reshape(shape_local)
    query_heads = split_heads(query_local, heads)
    key_heads = split_heads(key_local, heads)
    value_heads = split_heads(value_local, heads)
    total_start = (
        jnp.full((seq_count, heads, span_rows), NEGATIVE, jnp.float32),
        jnp.zeros((seq_count, heads, span_rows), jnp.float32),
    )
    accum_start = jnp.zeros((seq_count, heads, span_rows, head_size), jnp.float32)
    piece = lax.all_gather(key_local, "ctx", axis=1, tiled=True)
    block = math.gcd(piece.shape[1], 512)

    def total_inner(state, key_part):
        running, total = state
        key_block = split_heads(key_part, heads)
        scores = (
            jnp.einsum(
                "sqhd,skhd->shqk", query_heads, key_block, preferred_element_type=jnp.float32
            )
            * scale
        )
        newest = jnp.maximum(running, jnp.max(scores, -1))
        total = total * jnp.exp(running - newest) + jnp.sum(jnp.exp(scores - newest[..., None]), -1)
        return ((newest, total), None)

    result, unused = lax.scan(total_inner, total_start, row_blocks(piece, block))
    running, total = result
    log_total = running + jnp.log(total)
    piece = (
        lax.all_gather(key_local, "ctx", axis=1, tiled=True),
        lax.all_gather(value_local, "ctx", axis=1, tiled=True),
    )
    block = math.gcd(piece[0].shape[1], 512)

    def value_inner(accum, pair):
        key_block = split_heads(pair[0], heads)
        value_block = split_heads(pair[1], heads)
        scores = (
            jnp.einsum(
                "sqhd,skhd->shqk", query_heads, key_block, preferred_element_type=jnp.float32
            )
            * scale
        )
        weights = jnp.exp(scores - log_total[..., None]).astype(jnp.bfloat16)
        accum = accum + jnp.einsum(
            "shqk,skhd->shqd", weights, value_block, preferred_element_type=jnp.float32
        )
        return (accum, None)

    result, unused = lax.scan(
        value_inner, accum_start, (row_blocks(piece[0], block), row_blocks(piece[1], block))
    )
    accum = result
    attn_heads = jnp.moveaxis(accum, 1, 2)
    attn_rows = attn_heads.reshape(-1, width).astype(jnp.bfloat16)
    mixed = jnp.dot(attn_rows, proj_full, preferred_element_type=jnp.float32) + proj_bias
    first_sum = flat_input.astype(jnp.float32) + mixed
    normed, first_pull = jax.vjp(layer_norm, first_sum, attn_gain, attn_shift)
    normed_low = normed.astype(jnp.bfloat16)
    pre_act = jnp.dot(normed_low, up_full, preferred_element_type=jnp.float32) + up_bias
    activated, gelu_pull = jax.vjp(exact_gelu, pre_act)
    act_low = activated.astype(jnp.bfloat16)
    branch = jnp.dot(act_low, down_full, preferred_element_type=jnp.float32) + down_bias
    result_rows, second_pull = jax.vjp(layer_norm, normed + branch, ffn_gain, ffn_shift)
    layer_output = result_rows.reshape(shape_local)
    grad_out = cotangent.reshape(-1, width).astype(jnp.float32)
    grad_second, ffn_gain_grad, ffn_shift_grad = second_pull(grad_out)
    qkv_back, proj_back, up_back, down_back = (
        lax.all_gather(qkv_weight, "ctx", axis=0, tiled=True),
        lax.all_gather(proj_weight, "ctx", axis=0, tiled=True),
        lax.all_gather(up_weight, "ctx", axis=0, tiled=True),
        lax.all_gather(down_weight, "ctx", axis=0, tiled=True),
    )
    grad_branch = grad_second.astype(jnp.bfloat16)
    down_weight_local = left_dot(act_low, grad_branch)
    down_bias_grad = jnp.sum(grad_branch.astype(jnp.float32), 0)
    grad_act = right_dot(grad_branch, down_back)
    grad_pre = gelu_pull(grad_act)[0].astype(jnp.bfloat16)
    up_weight_local = left_dot(normed_low, grad_pre)
    up_bias_grad = jnp.sum(grad_pre.astype(jnp.float32), 0)
    grad_normed = grad_second + right_dot(grad_pre, up_back)
    grad_first, attn_gain_grad, attn_shift_grad = first_pull(grad_normed)
    grad_mixed = grad_first.astype(jnp.bfloat16)
    proj_weight_local = left_dot(attn_rows, grad_mixed)
    proj_bias_grad = jnp.sum(grad_mixed.astype(jnp.float32), 0)
    grad_attn = right_dot(grad_mixed, proj_back).astype(jnp.bfloat16).reshape(shape_local)
    grad_attn_heads = split_heads(grad_attn, heads)
    delta_local = jnp.sum(grad_attn_heads.astype(jnp.float32) * attn_heads, -1)
    delta_heads = jnp.moveaxis(delta_local, 2, 1)
    query_start = jnp.zeros((seq_count, span_rows, heads, head_size), jnp.float32)
    piece = (
        lax.all_gather(key_local, "ctx", axis=1, tiled=True),
        lax.all_gather(value_local, "ctx", axis=1, tiled=True),
    )
    block = math.gcd(piece[0].shape[1], 512)

    def query_inner(accum, pair):
        key_block = split_heads(pair[0], heads)
        value_block = split_heads(pair[1], heads)
        scores = (
            jnp.einsum(
                "sqhd,skhd->shqk", query_heads, key_block, preferred_element_type=jnp.float32
            )
            * scale
        )
        probs = jnp.exp(scores - log_total[..., None])
        grad_probs = jnp.einsum(
            "sqhd,skhd->shqk", grad_attn_heads, value_block, preferred_element_type=jnp.float32
        )
        grad_scores = (probs * (grad_probs - delta_heads[..., None])).astype(jnp.bfloat16)
        accum = (
            accum
            + jnp.einsum(
                "shqk,skhd->sqhd", grad_scores, key_block, preferred_element_type=jnp.float32
            )
            * scale
        )
        return (accum, None)

    result, unused = lax.scan(
        query_inner, query_start, (row_blocks(piece[0], block), row_blocks(piece[1], block))
    )
    grad_query = result
    lse_all, delta_all = (
        lax.all_gather(jnp.moveaxis(log_total, 1, 2), "ctx", axis=1, tiled=True),
        lax.all_gather(delta_local, "ctx", axis=1, tiled=True),
    )
    key_start = (
        jnp.zeros((seq_count, span_rows, heads, head_size), jnp.float32),
        jnp.zeros((seq_count, span_rows, heads, head_size), jnp.float32),
    )
    piece = (
        lax.all_gather(query_local, "ctx", axis=1, tiled=True),
        lax.all_gather(grad_attn, "ctx", axis=1, tiled=True),
    )
    count = piece[0].shape[1]
    block = math.gcd(count, 512)

    def key_inner(state, group):
        grad_key, grad_value = state
        query_block = split_heads(group[0], heads)
        grad_block = split_heads(group[1], heads)
        lse_block = jnp.moveaxis(group[2], 2, 1)
        delta_block = jnp.moveaxis(group[3], 2, 1)
        scores = (
            jnp.einsum(
                "sqhd,skhd->shqk", query_block, key_heads, preferred_element_type=jnp.float32
            )
            * scale
        )
        probs = jnp.exp(scores - lse_block[..., None])
        grad_value = grad_value + jnp.einsum(
            "shqk,sqhd->skhd",
            probs.astype(jnp.bfloat16),
            grad_block,
            preferred_element_type=jnp.float32,
        )
        grad_probs = jnp.einsum(
            "sqhd,skhd->shqk", grad_block, value_heads, preferred_element_type=jnp.float32
        )
        grad_scores = (probs * (grad_probs - delta_block[..., None])).astype(jnp.bfloat16)
        grad_key = (
            grad_key
            + jnp.einsum(
                "shqk,sqhd->skhd", grad_scores, query_block, preferred_element_type=jnp.float32
            )
            * scale
        )
        return ((grad_key, grad_value), None)

    members = (
        row_blocks(piece[0], block),
        row_blocks(piece[1], block),
        row_blocks(lse_all, block),
        row_blocks(delta_all, block),
    )
    result, unused = lax.scan(key_inner, key_start, members)
    grad_key, grad_value = result
    grad_query_rows = grad_query.reshape(-1, width).astype(jnp.bfloat16)
    grad_key_rows = grad_key.reshape(-1, width).astype(jnp.bfloat16)
    grad_value_rows = grad_value.reshape(-1, width).astype(jnp.bfloat16)
    grad_qkv = jnp.concatenate([grad_query_rows, grad_key_rows, grad_value_rows], 1)
    qkv_weight_local = left_dot(flat_input, grad_qkv)
    query_bias_grad = jnp.sum(grad_query_rows.astype(jnp.float32), 0)
    value_bias_grad = jnp.sum(grad_value_rows.astype(jnp.float32), 0)
    input_grad = (grad_first + right_dot(grad_qkv, qkv_back)).reshape(shape_local)
    shard_grads = (
        lax.psum_scatter(qkv_weight_local, "ctx", scatter_dimension=0, tiled=True),
        lax.psum_scatter(proj_weight_local, "ctx", scatter_dimension=0, tiled=True),
        lax.psum_scatter(up_weight_local, "ctx", scatter_dimension=0, tiled=True),
        lax.psum_scatter(down_weight_local, "ctx", scatter_dimension=0, tiled=True),
    )
    qkv_weight_grad, proj_weight_grad, up_weight_grad, down_weight_grad = lax.psum(
        (shard_grads[0], shard_grads[1], shard_grads[2], shard_grads[3]), "dp"
    )
    small_summed = lax.psum(
        (
            query_bias_grad,
            value_bias_grad,
            proj_bias_grad,
            attn_gain_grad,
            attn_shift_grad,
            up_bias_grad,
            down_bias_grad,
            ffn_gain_grad,
            ffn_shift_grad,
        ),
        ("dp", "ctx"),
    )
    return (
        layer_output,
        input_grad,
        qkv_weight_grad,
        small_summed[0],
        small_summed[1],
        proj_weight_grad,
        small_summed[2],
        small_summed[3],
        small_summed[4],
        up_weight_grad,
        small_summed[5],
        down_weight_grad,
        small_summed[6],
        small_summed[7],
        small_summed[8],
    )


def choose_plan(mesh):
    size = mesh.shape["ctx"]
    groups = mesh.shape["dp"]
    packed = size >= 4 and size & (size - 1) == 0 and HEADS % size == 0
    if not packed or groups != 4:
        return per_device
    return functools.partial(head_parallel, size, groups)


def exchange(values, size, bits):
    return lax.ppermute(values, "ctx", [(spot, spot ^ bits) for spot in range(size)])


def link_bits(size, turn):
    bits = []
    step = 2
    while step < size:
        bits.append(step)
        step *= 2
    return bits[::-1] if turn % 2 else bits


def near_labels(size, turn):
    labels = [0]
    for bit in link_bits(size, turn):
        labels = labels + [label | bit for label in labels]
    return labels


def gather_rows(pieces, size):
    whole = []
    for turn, held in enumerate(pieces):
        for bit in link_bits(size, turn):
            held = jnp.concatenate([held, exchange(held, size, bit)], 0)
        whole.append(held)
    near = jnp.concatenate(whole, 0)
    return near, exchange(near, size, 1)


def scatter_rows(near, far, count, size):
    total = near.astype(jnp.float32) + exchange(far, size, 1).astype(jnp.float32)
    total = total.astype(jnp.bfloat16)
    rows = total.shape[0] // count
    outs = []
    for turn in range(count):
        held = total[turn * rows : (turn + 1) * rows]
        bits = link_bits(size, turn)[::-1]
        for bit in bits:
            half = held.shape[0] // 2
            moved = exchange(held[half:], size, bit)
            held = held[:half].astype(jnp.float32) + moved.astype(jnp.float32)
            if bit != bits[-1]:
                held = held.astype(jnp.bfloat16)
        outs.append(held)
    return outs


def trade(blocks):
    return lax.all_to_all(blocks, "ctx", 0, 0)


def group_sum(values, chunks):
    spot = lax.axis_index("dp")
    end = (spot == 0) | (spot == 3)
    outs = []
    gate = None
    for piece in jnp.split(values, chunks, 0):
        if gate is not None:
            piece, gate = lax.optimization_barrier((piece, gate))
        got = lax.ppermute(piece, "dp", [(0, 1), (3, 2)])
        gate = got
        pair = (piece.astype(jnp.float32) + got.astype(jnp.float32)).astype(jnp.bfloat16)
        other = lax.ppermute(pair, "dp", [(1, 2), (2, 1)])
        total = (pair.astype(jnp.float32) + other.astype(jnp.float32)).astype(jnp.bfloat16)
        last = lax.ppermute(total, "dp", [(1, 0), (2, 3)])
        outs.append(jnp.where(end, last, total))
    return jnp.concatenate(outs, 0) if len(outs) > 1 else outs[0]


def small_sum(values, size, groups):
    step = 1
    while step < size:
        values = values + exchange(values, size, step)
        step *= 2
    step = 1
    while step < groups:
        values = values + lax.ppermute(values, "dp", [(g, g ^ step) for g in range(groups)])
        step *= 2
    return values


def attend_kernel(head_size, scale, table_ref, near_ref, far_ref, out_ref, lse_ref, qkv_ref):
    seq, step = pl.program_id(0), pl.program_id(1)
    half, lanes = near_ref.shape[0], near_ref.shape[1] // 3
    span = out_ref.shape[2]
    block = lse_ref.shape[2]
    head_of = lax.broadcasted_iota(jnp.int32, (1, lanes), 1) // head_size

    @pl.when(step == 0)
    def _():
        qkv_ref[0:half, :] = near_ref[...]
        qkv_ref[half:, :] = far_ref[...]

    query = qkv_ref[pl.ds(pl.multiple_of(step * block, block), block), 0:lanes]
    keys = qkv_ref[:, lanes : 2 * lanes]
    values = qkv_ref[:, 2 * lanes :]
    total = jnp.zeros((lanes, block), jnp.float32)
    for head in range(lanes // head_size):
        mine = head_of == head
        key = jnp.where(mine, keys, jnp.zeros_like(keys))
        value = jnp.where(mine, values, jnp.zeros_like(values))
        scores = right_dot(key, query) * scale
        top = jnp.max(scores, 0, keepdims=True)
        expo = jnp.exp(scores - top)
        norm = jnp.sum(expo, 0, keepdims=True)
        lse_ref[0, head : head + 1, :] = top + jnp.log(norm)
        total = total + left_dot(value, expo.astype(jnp.bfloat16)) / norm
    result = total.T.astype(jnp.bfloat16)
    count = block // span
    blocks = pl.num_programs(1) * count
    for spot in range(count):
        owner = table_ref[seq * blocks + step * count + spot]
        out_ref[owner, 0] = result[spot * span : (spot + 1) * span]


def attend(table, near, far, seqs, size, head_size, scale, block):
    half = near.shape[0] // seqs
    lanes = near.shape[1] // 3
    heads = lanes // head_size
    rows = 2 * half
    span = rows // size
    return pl.pallas_call(
        functools.partial(attend_kernel, head_size, scale),
        grid_spec=pltpu.PrefetchScalarGridSpec(
            num_scalar_prefetch=1,
            grid=(seqs, rows // block),
            in_specs=[
                pl.BlockSpec((half, 3 * lanes), lambda s, i, t: (s, 0)),
                pl.BlockSpec((half, 3 * lanes), lambda s, i, t: (s, 0)),
            ],
            out_specs=[
                pl.BlockSpec((size, 1, span, lanes), lambda s, i, t: (0, s, 0, 0)),
                pl.BlockSpec((1, heads, block), lambda s, i, t: (s, 0, i)),
            ],
            scratch_shapes=[pltpu.VMEM((rows, 3 * lanes), jnp.bfloat16)],
        ),
        out_shape=[
            jax.ShapeDtypeStruct((size, seqs, span, lanes), jnp.bfloat16),
            jax.ShapeDtypeStruct((seqs, heads, rows), jnp.float32),
        ],
        cost_estimate=pl.CostEstimate(
            flops=4 * seqs * rows * rows * lanes * heads,
            bytes_accessed=8 * seqs * rows * lanes,
            transcendentals=seqs * rows * rows * heads,
        ),
        name="attend",
    )(table, near, far)


def attend_back_kernel(
    head_size,
    scale,
    table_ref,
    near_ref,
    far_ref,
    lse_ref,
    grad_ref,
    near_out,
    far_out,
    qkv_ref,
    gq_ref,
    gk_ref,
    gv_ref,
):
    seq, step = pl.program_id(0), pl.program_id(1)
    half, lanes = near_ref.shape[0], near_ref.shape[1] // 3
    span = grad_ref.shape[2]
    block = lse_ref.shape[2]
    head_of = lax.broadcasted_iota(jnp.int32, (1, lanes), 1) // head_size

    @pl.when(step == 0)
    def _():
        qkv_ref[0:half, :] = near_ref[...]
        qkv_ref[half:, :] = far_ref[...]
        gk_ref[...] = jnp.zeros_like(gk_ref)
        gv_ref[...] = jnp.zeros_like(gv_ref)

    rows = pl.ds(pl.multiple_of(step * block, block), block)
    query = qkv_ref[rows, 0:lanes]
    keys = qkv_ref[:, lanes : 2 * lanes]
    values = qkv_ref[:, 2 * lanes :]
    count = block // span
    blocks = pl.num_programs(1) * count
    grad = jnp.concatenate(
        [grad_ref[table_ref[seq * blocks + step * count + spot], 0] for spot in range(count)], 0
    )
    total = jnp.zeros((lanes, block), jnp.float32)
    for head in range(lanes // head_size):
        mine = head_of == head
        key = jnp.where(mine, keys, jnp.zeros_like(keys))
        value = jnp.where(mine, values, jnp.zeros_like(values))
        query_head = jnp.where(mine, query, jnp.zeros_like(query))
        grad_head = jnp.where(mine, grad, jnp.zeros_like(grad))
        scores = right_dot(key, query) * scale
        probs = jnp.exp(scores - lse_ref[0, head : head + 1, :])
        grad_probs = right_dot(value, grad)
        gv_ref[...] += jnp.dot(
            probs.astype(jnp.bfloat16), grad_head, preferred_element_type=jnp.float32
        )
        delta = jnp.sum(probs * grad_probs, 0, keepdims=True)
        grad_scores = (probs * (grad_probs - delta)).astype(jnp.bfloat16)
        gk_ref[...] += jnp.dot(grad_scores, query_head, preferred_element_type=jnp.float32)
        total = total + left_dot(key, grad_scores)
    gq_ref[rows, :] = total.T * scale

    @pl.when(step == pl.num_programs(1) - 1)
    def _():
        for low, out in ((0, near_out), (half, far_out)):
            out[:, 0:lanes] = gq_ref[low : low + half, :].astype(jnp.bfloat16)
            out[:, lanes : 2 * lanes] = (gk_ref[low : low + half, :] * scale).astype(jnp.bfloat16)
            out[:, 2 * lanes :] = gv_ref[low : low + half, :].astype(jnp.bfloat16)


def attend_back(table, near, far, lse, grad, head_size, scale, block):
    size, seqs, span, lanes = grad.shape
    half = near.shape[0] // seqs
    heads = lanes // head_size
    rows = 2 * half
    return pl.pallas_call(
        functools.partial(attend_back_kernel, head_size, scale),
        grid_spec=pltpu.PrefetchScalarGridSpec(
            num_scalar_prefetch=1,
            grid=(seqs, rows // block),
            in_specs=[
                pl.BlockSpec((half, 3 * lanes), lambda s, i, t: (s, 0)),
                pl.BlockSpec((half, 3 * lanes), lambda s, i, t: (s, 0)),
                pl.BlockSpec((1, heads, block), lambda s, i, t: (s, 0, i)),
                pl.BlockSpec((size, 1, span, lanes), lambda s, i, t: (0, s, 0, 0)),
            ],
            out_specs=[
                pl.BlockSpec((half, 3 * lanes), lambda s, i, t: (s, 0)),
                pl.BlockSpec((half, 3 * lanes), lambda s, i, t: (s, 0)),
            ],
            scratch_shapes=[
                pltpu.VMEM((rows, 3 * lanes), jnp.bfloat16),
                pltpu.VMEM((rows, lanes), jnp.float32),
                pltpu.VMEM((rows, lanes), jnp.float32),
                pltpu.VMEM((rows, lanes), jnp.float32),
            ],
        ),
        out_shape=[
            jax.ShapeDtypeStruct((seqs * half, 3 * lanes), jnp.bfloat16),
            jax.ShapeDtypeStruct((seqs * half, 3 * lanes), jnp.bfloat16),
        ],
        cost_estimate=pl.CostEstimate(
            flops=10 * seqs * rows * rows * lanes * heads,
            bytes_accessed=16 * seqs * rows * lanes,
            transcendentals=seqs * rows * rows * heads,
        ),
        name="attend_back",
    )(table, near, far, lse, grad)


def norm_parts(values):
    center = values - jnp.mean(values, -1, keepdims=True)
    spread = jnp.mean(center * center, -1, keepdims=True)
    inverse = lax.rsqrt(spread + EPS)
    return center * inverse, inverse


def norm_back(grad, hat, inverse, gain):
    grad_hat = grad * gain
    first = jnp.mean(grad_hat, -1, keepdims=True)
    second = jnp.mean(grad_hat * hat, -1, keepdims=True)
    return inverse * (grad_hat - first - hat * second)


def gelu_pair(values):
    area = 0.5 * (1.0 + lax.erf(values * (0.5**0.5)))
    density = jnp.exp(-0.5 * values * values) * (1.0 / math.sqrt(2.0 * math.pi))
    return values * area, area + values * density


def to_bf16(values):
    return values.astype(jnp.bfloat16)


def head_parallel(
    size,
    groups,
    layer_input,
    qkv_weight,
    query_bias,
    value_bias,
    proj_weight,
    proj_bias,
    attn_gain,
    attn_shift,
    up_weight,
    up_bias,
    down_weight,
    down_bias,
    ffn_gain,
    ffn_shift,
    cotangent,
):
    me = lax.axis_index("ctx")
    seq_count, span_rows, width = layer_input.shape
    hidden = up_weight.shape[1]
    lanes = width // size
    part = hidden // size
    head_size = width // HEADS
    scale = head_size ** (-0.5)
    length = span_rows * size
    block = math.gcd(length, 256)
    rows = seq_count * span_rows
    flat = layer_input.reshape(rows, width)
    labels = []
    for turn in range(seq_count):
        near = near_labels(size, turn)
        labels += near + [label ^ 1 for label in near]
    table = jnp.bitwise_xor(jnp.array(labels, jnp.int32), me.astype(jnp.int32))

    def pieces(values):
        return [values[s * span_rows : (s + 1) * span_rows] for s in range(seq_count)]

    def scattered(near, far):
        return jnp.concatenate(scatter_rows(near, far, seq_count, size), 0)

    qkv_blocks = jnp.moveaxis(qkv_weight.reshape(-1, 3, size, lanes), 2, 0)
    qkv_mine = trade(qkv_blocks.reshape(size, -1, 3 * lanes)).reshape(width, 3 * lanes)
    inputs = gather_rows(pieces(flat), size)
    proj_all = lax.all_gather(proj_weight, "ctx", axis=0, tiled=True)
    up_blocks = jnp.moveaxis(up_weight.reshape(-1, size, part), 1, 0)
    up_mine = trade(up_blocks).reshape(width, part)
    qkv_bias = jnp.concatenate(
        [
            lax.dynamic_slice_in_dim(query_bias, me * lanes, lanes),
            jnp.zeros((lanes,), jnp.float32),
            lax.dynamic_slice_in_dim(value_bias, me * lanes, lanes),
        ]
    )
    up_bias_mine = lax.dynamic_slice_in_dim(up_bias, me * part, part)

    qkvs = [
        to_bf16(jnp.dot(side, qkv_mine, preferred_element_type=jnp.float32) + qkv_bias)
        for side in inputs
    ]
    attn, lse = attend(table, *qkvs, seq_count, size, head_size, scale, block)
    attn = jnp.moveaxis(trade(attn).reshape(size, rows, lanes), 0, 1).reshape(rows, width)

    mixed = jnp.dot(attn, proj_all, preferred_element_type=jnp.float32) + proj_bias
    first_hat, first_inverse = norm_parts(flat.astype(jnp.float32) + mixed)
    normed = first_hat * attn_gain + attn_shift
    lows = gather_rows(pieces(to_bf16(normed)), size)
    acts, slopes, branches = [], [], []
    for side in lows:
        pre = jnp.dot(side, up_mine, preferred_element_type=jnp.float32) + up_bias_mine
        act, slope = gelu_pair(pre)
        acts.append(to_bf16(act))
        slopes.append(to_bf16(slope))
        branches.append(to_bf16(jnp.dot(acts[-1], down_weight, preferred_element_type=jnp.float32)))
    branch = scattered(*branches) + down_bias

    hat, inverse = norm_parts(normed + branch)
    output = hat * ffn_gain + ffn_shift
    grad = cotangent.reshape(rows, width).astype(jnp.float32)
    second = norm_back(grad, hat, inverse, ffn_gain)
    grad_branch = to_bf16(second)
    small = [jnp.sum(grad * hat, 0), jnp.sum(grad, 0), jnp.sum(grad_branch.astype(jnp.float32), 0)]

    grad_sides = gather_rows(pieces(grad_branch), size)
    pres, partials = [], []
    for side, slope in zip(grad_sides, slopes):
        pre = to_bf16(right_dot(side, down_weight) * slope.astype(jnp.float32))
        pres.append(pre)
        partials.append(to_bf16(right_dot(pre, up_mine)))
    grad_normed = second + scattered(*partials)
    down_grad = sum(left_dot(act, side) for act, side in zip(acts, grad_sides))
    up_grad = sum(left_dot(low, pre) for low, pre in zip(lows, pres))
    up_bias_part = sum(jnp.sum(pre.astype(jnp.float32), 0) for pre in pres)

    down_weight_grad = lax.psum(to_bf16(down_grad), "dp").astype(jnp.float32)
    up_weight_grad = lax.psum(trade(to_bf16(up_grad).reshape(size, -1, part)), "dp")
    up_weight_grad = jnp.moveaxis(up_weight_grad, 0, 1).reshape(-1, hidden).astype(jnp.float32)

    first = norm_back(grad_normed, first_hat, first_inverse, attn_gain)
    grad_mixed = to_bf16(first)
    small += [
        jnp.sum(grad_normed * first_hat, 0),
        jnp.sum(grad_normed, 0),
        jnp.sum(grad_mixed.astype(jnp.float32), 0),
    ]
    grad_attn = to_bf16(right_dot(grad_mixed, proj_all)).reshape(rows, size, lanes)
    grad_attn = trade(jnp.moveaxis(grad_attn, 1, 0).reshape(size, seq_count, span_rows, lanes))
    proj_part = lax.psum_scatter(
        to_bf16(left_dot(attn, grad_mixed)), "ctx", scatter_dimension=0, tiled=True
    )
    proj_weight_grad = group_sum(proj_part, 1).astype(jnp.float32)

    grad_qkvs = attend_back(table, *qkvs, lse, grad_attn, head_size, scale, block)
    qkv_grad = sum(left_dot(side, grads) for side, grads in zip(inputs, grad_qkvs))
    qkv_traded = trade(to_bf16(qkv_grad).reshape(size, -1, 3 * lanes))
    qkv_weight_grad = group_sum(qkv_traded, 2)
    qkv_weight_grad = jnp.moveaxis(qkv_weight_grad.reshape(size, -1, 3, lanes), 0, 2)
    qkv_weight_grad = qkv_weight_grad.reshape(-1, 3 * width).astype(jnp.float32)
    input_grad = first + scattered(*[to_bf16(right_dot(grads, qkv_mine)) for grads in grad_qkvs])
    bias_part = sum(jnp.sum(grads.astype(jnp.float32), 0) for grads in grad_qkvs)

    def placed(values, count):
        return lax.dynamic_update_slice(
            jnp.zeros((count,), jnp.float32), values, (me * values.shape[0],)
        )

    sums = jnp.concatenate(
        small
        + [
            placed(up_bias_part, hidden),
            placed(bias_part[:lanes], width),
            placed(bias_part[2 * lanes :], width),
        ]
    )
    sums = small_sum(sums.reshape(-1, 128), size, groups).reshape(-1)
    kept = [sums[k * width : (k + 1) * width] for k in range(6)]
    rest = sums[6 * width :]
    shape_local = (seq_count, span_rows, width)
    return (
        output.reshape(shape_local),
        input_grad.reshape(shape_local),
        qkv_weight_grad,
        rest[hidden : hidden + width],
        rest[hidden + width :],
        proj_weight_grad,
        kept[5],
        kept[3],
        kept[4],
        up_weight_grad,
        rest[:hidden],
        down_weight_grad,
        kept[2],
        kept[0],
        kept[1],
    )


def solution(mesh):
    return jax.shard_map(
        choose_plan(mesh),
        mesh=mesh,
        in_specs=(
            P("dp", "ctx", None),
            P("ctx", None),
            P(),
            P(),
            P("ctx", None),
            P(),
            P(),
            P(),
            P("ctx", None),
            P(),
            P("ctx", None),
            P(),
            P(),
            P(),
            P("dp", "ctx", None),
        ),
        out_specs=(
            P("dp", "ctx", None),
            P("dp", "ctx", None),
            P("ctx", None),
            P(),
            P(),
            P("ctx", None),
            P(),
            P(),
            P(),
            P("ctx", None),
            P(),
            P("ctx", None),
            P(),
            P(),
            P(),
        ),
        check_vma=False,
    )
```
